512 devices in a mesh: section: 64 (over y, z), head: 8 (over x, core).
Axes of the slice: x: 4, y: 4, z: 16, core: 2. Of those that a mesh axis runs over, the one named last changes fastest.
Arguments:
- queries: bfloat16 [12288, 4096], P('section', 'head'), may hold values from -20 to 20
- keys: bfloat16 [12288, 1024], P('section', 'head'), may hold values from -20 to 20
- values: bfloat16 [12288, 1024], P('section', 'head'), may hold values from -6 to 6
- d_attn: bfloat16 [12288, 4096], P('section', 'head'), may hold values from -72 to 72
- d_out: bfloat16 [12288, 4096], P('section', 'head'), may hold values from -6 to 6
- w_query: bfloat16 [4096, 4096], P(None, 'head'), may hold values from -0.09375 to 0.09375
- prefix_len: int32 [64], replicated, may hold values from 0 to 12096, as said below
Outputs:
- grad_prev: bfloat16 [12288, 4096], P('section', 'head')
The draws below stay inside these ranges and needn't reach their ends.
Inputs may be any that keep to these rules, and one draw needn't show every extreme that they name: prefix_len[s] <= s * 192 for every slice s; the first slice's is 0 and the last slice's is 12096.
All inputs are finite; a program needn't handle non-finite values.
Results may differ from the reference program's by a relative error of at most 0.035.
Values may be sent and summed in bfloat16 or wider, within the bound.
No kernel may reach another device: no remote copies, remote signals or barrier semaphores. Data moves between devices by JAX's collectives and lax.ppermute only.
A program may use at most 64 MiB of HBM per device.

```python
import jax
import jax.numpy as jnp
from jax import lax

D = 4096
HEAD_DIM = 128
QH_DEV = 4
ROWS = 192
SLICES = 64
TOKENS = 12288
KV_HEADS = 8
QHEADS = 32
LMAX = 12096


def draw_queries(key, part):
    base_draw = jnp.clip(jax.random.normal(jax.random.fold_in(key, 11), (TOKENS, QHEADS * HEAD_DIM), jnp.float32), -5.0, 5.0)
    return base_draw.astype(jnp.bfloat16)


def draw_keys(key, part):
    base_draw = jnp.clip(jax.random.normal(jax.random.fold_in(key, 13), (TOKENS, KV_HEADS * HEAD_DIM), jnp.float32), -5.0, 5.0)
    return base_draw.astype(jnp.bfloat16)


def draw_prefix_len(key, part):
    slice_id = jnp.arange(SLICES, dtype=jnp.int32)
    reach_keys = jnp.minimum(slice_id * ROWS, LMAX)
    drawn = jax.random.randint(jax.random.fold_in(key, 17), (SLICES,), 0, reach_keys + 1, dtype=jnp.int32)
    return jnp.where(slice_id == SLICES - 1, LMAX, drawn).astype(jnp.int32)


def block_scale(own_key, dims, cuts, low, high):
    gain = 1.0
    for dim, shards_of in cuts:
        steps = jax.random.uniform(jax.random.fold_in(jax.random.fold_in(own_key, 6), dim), (shards_of,), jnp.float32, low / len(cuts), high / len(cuts))
        gain = gain * jnp.repeat(jnp.exp(steps), dims[dim] // shards_of).reshape((-1,) + (1,) * (len(dims) - 1 - dim))
    return gain


def noise(rng, dims, width, reach, split=(), kind=jnp.bfloat16):
    array = width * jax.random.normal(rng, dims, jnp.float32)
    if split:
        array = array * block_scale(rng, dims, split, -0.22, 0.18)
    return jnp.clip(array, -reach, reach).astype(kind)


def setup_inputs(seed: int = 0) -> dict:
    key_of = jax.random.split(jax.random.key(seed), 8)
    queries = draw_queries(jax.random.fold_in(key_of[7], 71), 0)
    keys = draw_keys(jax.random.fold_in(key_of[7], 71), 0)
    values = noise(key_of[2], (TOKENS, KV_HEADS * HEAD_DIM), 1.0, 6.0, ((0, 64), (1, 8)))
    d_attn = noise(key_of[3], (TOKENS, QHEADS * HEAD_DIM), 12.0, 72.0, ((0, 64), (1, 8)))
    d_out = noise(key_of[4], (TOKENS, D), 1.0, 6.0, ((0, 64), (1, 8)))
    w_query = noise(key_of[5], (D, QHEADS * HEAD_DIM), D ** -0.5, 0.09375, ((1, 8),))
    prefix_len = draw_prefix_len(jax.random.fold_in(key_of[7], 71), 0)
    return {"queries": queries, "keys": keys, "values": values, "d_attn": d_attn, "d_out": d_out, "w_query": w_query, "prefix_len": prefix_len}


masked_score = -1.0e30


def slice_gradient(slice_id, queries, keys, values, d_attn, d_out, w_query, prefix_len):
    window = LMAX + ROWS
    base_row = (slice_id * ROWS).astype(jnp.int32)
    window_start = jnp.maximum(base_row - LMAX, 0).astype(jnp.int32)
    lower_key = base_row - prefix_len[slice_id]
    positions = base_row + jnp.arange(ROWS, dtype=jnp.int32)
    key_position = window_start + jnp.arange(window, dtype=jnp.int32)
    allowed = (key_position[None, :] >= lower_key) & (key_position[None, :] <= positions[:, None])
    score_scale = HEAD_DIM ** -0.5
    group_width = QH_DEV * HEAD_DIM
    zero_index = jnp.int32(0)

    def add_group(group_index, running_total):
        group_index = group_index.astype(jnp.int32)
        column = (group_index * group_width).astype(jnp.int32)
        kv_column = (group_index * HEAD_DIM).astype(jnp.int32)
        query_block = lax.dynamic_slice(queries, (base_row, column), (ROWS, group_width))
        grad_block = lax.dynamic_slice(d_attn, (base_row, column), (ROWS, group_width))
        query_float = query_block.astype(jnp.float32).reshape(ROWS, QH_DEV, HEAD_DIM)
        grad_float = grad_block.astype(jnp.float32).reshape(ROWS, QH_DEV, HEAD_DIM)
        key_float = lax.dynamic_slice(keys, (window_start, kv_column), (window, HEAD_DIM)).astype(jnp.float32)
        value_float = lax.dynamic_slice(values, (window_start, kv_column), (window, HEAD_DIM)).astype(jnp.float32)
        scores = jnp.einsum("rjd,ud->jru", query_float, key_float, precision=lax.Precision.HIGHEST) * score_scale
        scores = jnp.where(allowed[None], scores, masked_score)
        row_max = jnp.max(scores, axis=2, keepdims=True)
        weights = jnp.where(allowed[None], jnp.exp(scores - row_max), 0.0)
        probability = weights / jnp.sum(weights, axis=2, keepdims=True)
        grad_prob = jnp.einsum("rjd,ud->jru", grad_float, value_float, precision=lax.Precision.HIGHEST)
        delta_rows = jnp.sum(probability * grad_prob, axis=2, keepdims=True)
        weighted_low = (probability * grad_prob).astype(jnp.bfloat16).astype(jnp.float32)
        probs_low = probability.astype(jnp.bfloat16).astype(jnp.float32)
        weighted_keys = jnp.einsum("jru,ud->jrd", weighted_low, key_float, precision=lax.Precision.HIGHEST)
        prob_keys = jnp.einsum("jru,ud->jrd", probs_low, key_float, precision=lax.Precision.HIGHEST)
        grad_query = (weighted_keys - delta_rows * prob_keys) * score_scale
        grad_query = grad_query.transpose(1, 0, 2).reshape(ROWS, group_width).astype(jnp.bfloat16)
        weight_block = lax.dynamic_slice(w_query, (zero_index, column), (D, group_width))
        partial_sum = lax.dot_general(grad_query, weight_block, (((1,), (1,)), ((), ())), preferred_element_type=jnp.float32)
        return running_total + partial_sum.astype(jnp.bfloat16).astype(jnp.float32)

    running_total = lax.fori_loop(0, KV_HEADS, add_group, jnp.zeros((ROWS, D), jnp.float32))
    own_out = lax.dynamic_slice(d_out, (base_row, zero_index), (ROWS, D))
    return (own_out.astype(jnp.float32) + running_total).astype(jnp.bfloat16)


def reference(queries, keys, values, d_attn, d_out, w_query, prefix_len):
    def one_slice(slice_id):
        return slice_gradient(slice_id, queries, keys, values, d_attn, d_out, w_query, prefix_len)

    hidden = lax.map(one_slice, jnp.arange(SLICES, dtype=jnp.int32))
    hidden = hidden.reshape(TOKENS, D)
    return jnp.concatenate([hidden[ROWS:], jnp.zeros((ROWS, D), jnp.bfloat16)], axis=0)
```

```python
import functools
import math

import jax
import jax.numpy as jnp
from jax import lax
from jax.experimental import pallas as pl
from jax.experimental.pallas import tpu as pltpu
from jax.sharding import Mesh, PartitionSpec as P


ROWS = 192
WIDTH = 128
HEADS = 4
SLOTS = HEADS * ROWS
LOW = -1e30
SLACK = 8.0
SCALE = WIDTH ** -0.5
Y, Z, X, C = 4, 16, 4, 2


def attend(counts, group, offset, first, last, par_ref, pos_ref, *refs):
    refs = list(refs)
    q_ref, g_ref = refs[:2]
    kv_refs = refs[2 : 2 + len(counts)]
    refs = refs[2 + len(counts) :]
    if not first:
        sw_in, sp_in, st_in = refs[:3]
        refs = refs[3:]
    outs = refs[: 1 if last else 3]
    slot_pos, buf, q_s, g_s, m_s, w_s, p_s = refs[1 if last else 3 :]
    base = par_ref[0]
    lo = par_ref[1]

    for h in range(HEADS):
        rows = pl.ds(h * ROWS, ROWS)
        cols = pl.ds(h * WIDTH, WIDTH)
        scaled = q_ref[:, cols].astype(jnp.float32) * (SCALE * math.log2(math.e))
        high = scaled.astype(jnp.bfloat16)
        q_s[rows, :WIDTH] = high
        q_s[rows, WIDTH:] = (scaled - high.astype(jnp.float32)).astype(jnp.bfloat16)
        g_s[rows, :] = g_ref[:, cols]
    if first:
        m_s[...] = jnp.full((SLOTS, WIDTH), LOW, jnp.float32)
        w_s[...] = jnp.zeros((SLOTS, 2 * WIDTH), jnp.float32)
        p_s[...] = jnp.zeros((SLOTS, 2 * WIDTH), jnp.float32)
    else:
        st = st_in[...]
        shape = (SLOTS, WIDTH)
        m_s[...] = jnp.broadcast_to(st[:, 0:1], shape)
        p_s[:, :WIDTH] = sp_in[...]
        p_s[:, WIDTH:] = jnp.broadcast_to(st[:, 64:65], shape)
        w_s[:, :WIDTH] = sw_in[...]
        w_s[:, WIDTH:] = jnp.broadcast_to(st[:, 127:128], shape)

    def collect(used, chosen_of):
        at = offset
        for ref, n in zip(kv_refs, counts):

            def place(j, slot, ref=ref, at=at):
                p = pos_ref[at + j]
                chosen = chosen_of(p)

                @pl.when(chosen)
                def _():
                    buf[slot] = ref[j]
                    slot_pos[slot] = p

                return slot + chosen.astype(jnp.int32)

            used = lax.fori_loop(0, n, place, used)
            at += n
        return used

    full = collect(jnp.int32(0), lambda p: (p >= lo) & (p < base))
    used = collect(
        full, lambda p: (p + ROWS > lo) & (p <= base) & ((p < lo) | (p == base))
    )
    groups = (used + group - 1) // group
    for j in range(group - 1):

        @pl.when(used + j < groups * group)
        def _():
            buf[used + j] = jnp.zeros((ROWS, 2 * WIDTH), jnp.bfloat16)
            slot_pos[used + j] = jnp.int32(1 << 30)

    contract = (((1,), (1,)), ((), ()))

    def visit(g, rows, masked):
        start = g * group
        kv = jnp.concatenate([buf[start + j] for j in range(group)], axis=0)
        k, v = kv[:, :WIDTH], kv[:, WIDTH:]
        kk = jnp.concatenate([k, k], axis=1)
        k1 = jnp.concatenate([k, jnp.ones_like(k)], axis=1)
        s = lax.dot_general(q_s[rows, :], kk, contract, preferred_element_type=jnp.float32)
        if masked:
            lane = lax.broadcasted_iota(jnp.int32, (1, ROWS), 1)
            key_at = jnp.concatenate([lane + slot_pos[start + j] for j in range(group)], axis=1)
            row = lax.broadcasted_iota(jnp.int32, (ROWS, group * ROWS), 0) + base
            inside = (key_at >= lo) & (key_at <= row)
            s = jnp.where(inside, s, LOW)
        top = jnp.max(s, axis=1, keepdims=True)

        @pl.when(jnp.max(top - m_s[rows, 0:1]) > SLACK)
        def _():
            old = m_s[rows, :]
            new = jnp.maximum(old, top)
            factor = jnp.exp2(old - new)[:, 0:1]
            m_s[rows, :] = new
            w_s[rows, :] = w_s[rows, :] * factor
            p_s[rows, :] = p_s[rows, :] * factor

        prob = jnp.exp2(s - m_s[rows, 0:1])
        if masked:
            prob = jnp.where(inside, prob, 0.0)
        dp = lax.dot_general(g_s[rows, :], v, contract, preferred_element_type=jnp.float32)
        w_s[rows, :] += jnp.dot(
            (prob * dp).astype(jnp.bfloat16), k1, preferred_element_type=jnp.float32
        )
        p_s[rows, :] += jnp.dot(prob.astype(jnp.bfloat16), k1, preferred_element_type=jnp.float32)

    @pl.loop(0, groups)
    def _(g):
        whole = (g + 1) * group <= full
        pl.when(whole)(lambda: visit(g, pl.ds(0, SLOTS), False))

        @pl.when(jnp.logical_not(whole))
        def _():
            @pl.loop(0, HEADS)
            def _(h):
                visit(g, pl.ds(pl.multiple_of(h * ROWS, ROWS), ROWS), True)

    if last:
        l = p_s[:, WIDTH:]
        l = jnp.where(l > 0.0, l, 1.0)
        delta = w_s[:, WIDTH:] / l
        grad = (w_s[:, :WIDTH] - delta * p_s[:, :WIDTH]) / l * SCALE
        for h in range(HEADS):
            outs[0][:, pl.ds(h * WIDTH, WIDTH)] = grad[h * ROWS : (h + 1) * ROWS].astype(jnp.bfloat16)
    else:
        sw_out, sp_out, st_out = outs
        sw_out[...] = w_s[:, :WIDTH]
        sp_out[...] = p_s[:, :WIDTH]
        lane = lax.broadcasted_iota(jnp.int32, (SLOTS, WIDTH), 1)
        st_out[...] = jnp.where(
            lane < 43, m_s[...], jnp.where(lane < 86, p_s[:, WIDTH:], w_s[:, WIDTH:])
        )


def attention(par, pos, offset, q, g, arrays, state, last):
    counts = tuple(a.shape[0] for a in arrays)
    first = state is None
    total = sum(counts)
    group = {4: 4, 12: 6}.get(total, 8)
    shape = jax.ShapeDtypeStruct((SLOTS, WIDTH), jnp.float32)
    out_shape = jax.ShapeDtypeStruct((ROWS, HEADS * WIDTH), jnp.bfloat16) if last else [shape] * 3
    operands = [q, g, *arrays] + ([] if first else list(state))
    vmem = pl.BlockSpec(memory_space=pltpu.VMEM)
    smem = pl.BlockSpec(memory_space=pltpu.SMEM)
    return pl.pallas_call(
        functools.partial(attend, counts, group, offset, first, last),
        in_specs=[smem, smem] + [vmem] * len(operands),
        out_specs=vmem if last else [vmem] * 3,
        out_shape=out_shape,
        scratch_shapes=[
            pltpu.SMEM((total + group,), jnp.int32),
            pltpu.VMEM((total + group, ROWS, 2 * WIDTH), jnp.bfloat16),
            pltpu.VMEM((SLOTS, 2 * WIDTH), jnp.bfloat16),
            pltpu.VMEM((SLOTS, WIDTH), jnp.bfloat16),
            pltpu.VMEM((SLOTS, WIDTH), jnp.float32),
            pltpu.VMEM((SLOTS, 2 * WIDTH), jnp.float32),
            pltpu.VMEM((SLOTS, 2 * WIDTH), jnp.float32),
        ],
        compiler_params=pltpu.CompilerParams(vmem_limit_bytes=24 << 20),
        cost_estimate=pl.CostEstimate(
            flops=8 * total * ROWS * SLOTS * WIDTH // 2,
            transcendentals=total * ROWS * SLOTS // 2,
            bytes_accessed=total * ROWS * 2 * WIDTH * 2 + 3 * SLOTS * WIDTH * 8,
        ),
        name="attend",
    )(par, pos, *operands)


def project_body(index_ref, gq_ref, w_ref, out_ref):
    grad_query = gq_ref[...]
    width = grad_query.shape[1]
    for i in range(X):
        block = pl.ds(pl.multiple_of(index_ref[i] * width, width), width)
        out_ref[i] = lax.dot_general(
            grad_query,
            w_ref[block, :],
            (((1,), (1,)), ((), ())),
            preferred_element_type=jnp.float32,
        ).astype(jnp.bfloat16)


def project(index, grad_query, w_query):
    vmem = pl.BlockSpec(memory_space=pltpu.VMEM)
    return pl.pallas_call(
        project_body,
        in_specs=[pl.BlockSpec(memory_space=pltpu.SMEM), vmem, vmem],
        out_specs=vmem,
        out_shape=jax.ShapeDtypeStruct((X, ROWS, grad_query.shape[1]), jnp.bfloat16),
        compiler_params=pltpu.CompilerParams(vmem_limit_bytes=16 << 20),
        name="project",
    )(index, grad_query, w_query)


def exchange(value, axis, mask):
    count = lax.axis_size(axis)
    return lax.ppermute(value, axis, [(i, i ^ mask) for i in range(count)])


def add(a, b):
    return (a.astype(jnp.float32) + b.astype(jnp.float32)).astype(jnp.bfloat16)


def reduce_heads(grad_query, w_query, d_out):
    x_id = lax.axis_index("x")
    core = lax.axis_index("core")
    order = jnp.arange(X, dtype=jnp.int32)
    order = x_id ^ (order ^ (order >> 1))
    sent = exchange(project(order * C + (1 - core), grad_query, w_query), "core", 1)
    held = add(project(order * C + core, grad_query, w_query), sent)
    total = held[0].astype(jnp.float32) + d_out.astype(jnp.float32)
    for i, mask in ((3, 2), (1, 1), (2, 3)):
        total = total + exchange(held[i], "x", mask).astype(jnp.float32)
    return total.astype(jnp.bfloat16)


def shards(queries, keys, values, d_attn, d_out, w_query, prefix_len):
    y_id = lax.axis_index("y")
    z_id = lax.axis_index("z")
    owner = y_id * Z + z_id + 1
    base = owner * ROWS
    reach = prefix_len[jnp.minimum(owner, Y * Z - 1)]
    lo = jnp.where(owner < Y * Z, jnp.maximum(base - reach, 0), 1 << 28)
    par = jnp.where(jnp.arange(2) == 0, base, lo).astype(jnp.int32)

    own = jnp.concatenate([queries, d_attn, d_out], axis=1)
    own = lax.ppermute(own, ("y", "z"), [(i + 1, i) for i in range(Y * Z - 1)])
    width = queries.shape[1]
    q, g, d_out = own[:, :width], own[:, width : 2 * width], own[:, 2 * width :]

    mine = lax.all_gather(jnp.concatenate([keys, values], axis=1), "y", axis=0)

    up = [(z, (z + 1) % Z) for z in range(Z)]
    down = [(z, (z - 1) % Z) for z in range(Z)]

    turn = jnp.arange(Z * Y, dtype=jnp.int32)
    hop = turn // Y
    hop = jnp.where(hop % 2 == 1, (hop + 1) // 2, Z - hop // 2)
    pos = ((z_id + Z - hop) % Z + turn % Y * Z) * ROWS

    half = Z // 2
    below = above = mine
    arrays, done = [mine], 0
    state = None
    for step in range(1, half + 1):
        last = step == half
        below = lax.ppermute(below[: Y // 2] if last else below, "z", up)
        above = lax.ppermute(above[Y // 2 :] if last else above, "z", down)
        if step % 2 == 0:
            state = attention(par, pos, done, q, g, arrays, state, False)
            done += sum(a.shape[0] for a in arrays)
            arrays = []
        arrays += [below, above]
    state = attention(par, pos, done, q, g, arrays, state, True)
    return reduce_heads(state, w_query, d_out)


def solution(mesh):
    fine = Mesh(mesh.devices.reshape(Y, Z, X, C), ("y", "z", "x", "core"))
    split = P(("y", "z"), ("x", "core"))
    placed = (split, split, split, split, split, P(None, ("x", "core")), P())

    return jax.shard_map(shards, mesh=fine, in_specs=placed, out_specs=split, check_vma=False)
```

```python
import functools
import math

import jax
import jax.numpy as jnp
from jax import lax
from jax.experimental import pallas as pl
from jax.experimental.pallas import tpu as pltpu
from jax.sharding import Mesh, PartitionSpec as P


ROWS = 192
WIDTH = 128
HEADS = 4
SLOTS = HEADS * ROWS
LOW = -1e30
SLACK = 8.0
SCALE = WIDTH ** -0.5
Y, Z, X, C = 4, 16, 4, 2


def attend(counts, group, offset, first, last, par_ref, pos_ref, *refs):
    refs = list(refs)
    q_ref, g_ref = refs[:2]
    kv_refs = refs[2 : 2 + len(counts)]
    refs = refs[2 + len(counts) :]
    if not first:
        sw_in, sp_in, st_in = refs[:3]
        refs = refs[3:]
    outs = refs[: 1 if last else 3]
    slot_pos, buf, q_s, g_s, m_s, w_s, p_s = refs[1 if last else 3 :]
    base = par_ref[0]
    lo = par_ref[1]

    for h in range(HEADS):
        rows = pl.ds(h * ROWS, ROWS)
        cols = pl.ds(h * WIDTH, WIDTH)
        scaled = q_ref[:, cols].astype(jnp.float32) * (SCALE * math.log2(math.e))
        high = scaled.astype(jnp.bfloat16)
        q_s[rows, :WIDTH] = high
        q_s[rows, WIDTH:] = (scaled - high.astype(jnp.float32)).astype(jnp.bfloat16)
        g_s[rows, :] = g_ref[:, cols]
    if first:
        m_s[...] = jnp.full((SLOTS, WIDTH), LOW, jnp.float32)
        w_s[...] = jnp.zeros((SLOTS, 2 * WIDTH), jnp.float32)
        p_s[...] = jnp.zeros((SLOTS, 2 * WIDTH), jnp.float32)
    else:
        st = st_in[...]
        shape = (SLOTS, WIDTH)
        m_s[...] = jnp.broadcast_to(st[:, 0:1], shape)
        p_s[:, :WIDTH] = sp_in[...]
        p_s[:, WIDTH:] = jnp.broadcast_to(st[:, 64:65], shape)
        w_s[:, :WIDTH] = sw_in[...]
        w_s[:, WIDTH:] = jnp.broadcast_to(st[:, 127:128], shape)

    def collect(used, chosen_of):
        at = offset
        for ref, n in zip(kv_refs, counts):

            def place(j, slot, ref=ref, at=at):
                p = pos_ref[at + j]
                chosen = chosen_of(p)

                @pl.when(chosen)
                def _():
                    buf[slot] = ref[j]
                    slot_pos[slot] = p

                return slot + chosen.astype(jnp.int32)

            used = lax.fori_loop(0, n, place, used)
            at += n
        return used

    full = collect(jnp.int32(0), lambda p: (p >= lo) & (p < base))
    used = collect(
        full, lambda p: (p + ROWS > lo) & (p <= base) & ((p < lo) | (p == base))
    )
    groups = (used + group - 1) // group
    for j in range(group - 1):

        @pl.when(used + j < groups * group)
        def _():
            buf[used + j] = jnp.zeros((ROWS, 2 * WIDTH), jnp.bfloat16)
            slot_pos[used + j] = jnp.int32(1 << 30)

    contract = (((1,), (1,)), ((), ()))

    def visit(g, rows, masked):
        start = g * group
        kv = jnp.concatenate([buf[start + j] for j in range(group)], axis=0)
        k, v = kv[:, :WIDTH], kv[:, WIDTH:]
        kk = jnp.concatenate([k, k], axis=1)
        k1 = jnp.concatenate([k, jnp.ones_like(k)], axis=1)
        s = lax.dot_general(q_s[rows, :], kk, contract, preferred_element_type=jnp.float32)
        if masked:
            lane = lax.broadcasted_iota(jnp.int32, (1, ROWS), 1)
            key_at = jnp.concatenate([lane + slot_pos[start + j] for j in range(group)], axis=1)
            row = lax.broadcasted_iota(jnp.int32, (ROWS, group * ROWS), 0) + base
            inside = (key_at >= lo) & (key_at <= row)
            s = jnp.where(inside, s, LOW)
        top = jnp.max(s, axis=1, keepdims=True)

        @pl.when(jnp.max(top - m_s[rows, 0:1]) > SLACK)
        def _():
            old = m_s[rows, :]
            new = jnp.maximum(old, top)
            factor = jnp.exp2(old - new)[:, 0:1]
            m_s[rows, :] = new
            w_s[rows, :] = w_s[rows, :] * factor
            p_s[rows, :] = p_s[rows, :] * factor

        prob = jnp.exp2(s - m_s[rows, 0:1])
        if masked:
            prob = jnp.where(inside, prob, 0.0)
        dp = lax.dot_general(g_s[rows, :], v, contract, preferred_element_type=jnp.float32)
        w_s[rows, :] += jnp.dot(
            (prob * dp).astype(jnp.bfloat16), k1, preferred_element_type=jnp.float32
        )
        p_s[rows, :] += jnp.dot(prob.astype(jnp.bfloat16), k1, preferred_element_type=jnp.float32)

    @pl.loop(0, groups)
    def _(g):
        whole = (g + 1) * group <= full
        pl.when(whole)(lambda: visit(g, pl.ds(0, SLOTS), False))

        @pl.when(jnp.logical_not(whole))
        def _():
            @pl.loop(0, HEADS)
            def _(h):
                visit(g, pl.ds(pl.multiple_of(h * ROWS, ROWS), ROWS), True)

    if last:
        l = p_s[:, WIDTH:]
        l = jnp.where(l > 0.0, l, 1.0)
        delta = w_s[:, WIDTH:] / l
        grad = (w_s[:, :WIDTH] - delta * p_s[:, :WIDTH]) / l * SCALE
        for h in range(HEADS):
            outs[0][:, pl.ds(h * WIDTH, WIDTH)] = grad[h * ROWS : (h + 1) * ROWS].astype(jnp.bfloat16)
    else:
        sw_out, sp_out, st_out = outs
        sw_out[...] = w_s[:, :WIDTH]
        sp_out[...] = p_s[:, :WIDTH]
        lane = lax.broadcasted_iota(jnp.int32, (SLOTS, WIDTH), 1)
        st_out[...] = jnp.where(
            lane < 43, m_s[...], jnp.where(lane < 86, p_s[:, WIDTH:], w_s[:, WIDTH:])
        )


def attention(par, pos, offset, q, g, arrays, state, last):
    counts = tuple(a.shape[0] for a in arrays)
    first = state is None
    total = sum(counts)
    group = {4: 4, 12: 6}.get(total, 8)
    shape = jax.ShapeDtypeStruct((SLOTS, WIDTH), jnp.float32)
    out_shape = jax.ShapeDtypeStruct((ROWS, HEADS * WIDTH), jnp.bfloat16) if last else [shape] * 3
    operands = [q, g, *arrays] + ([] if first else list(state))
    vmem = pl.BlockSpec(memory_space=pltpu.VMEM)
    smem = pl.BlockSpec(memory_space=pltpu.SMEM)
    return pl.pallas_call(
        functools.partial(attend, counts, group, offset, first, last),
        in_specs=[smem, smem] + [vmem] * len(operands),
        out_specs=vmem if last else [vmem] * 3,
        out_shape=out_shape,
        scratch_shapes=[
            pltpu.SMEM((total + group,), jnp.int32),
            pltpu.VMEM((total + group, ROWS, 2 * WIDTH), jnp.bfloat16),
            pltpu.VMEM((SLOTS, 2 * WIDTH), jnp.bfloat16),
            pltpu.VMEM((SLOTS, WIDTH), jnp.bfloat16),
            pltpu.VMEM((SLOTS, WIDTH), jnp.float32),
            pltpu.VMEM((SLOTS, 2 * WIDTH), jnp.float32),
            pltpu.VMEM((SLOTS, 2 * WIDTH), jnp.float32),
        ],
        compiler_params=pltpu.CompilerParams(vmem_limit_bytes=24 << 20),
        cost_estimate=pl.CostEstimate(
            flops=8 * total * ROWS * SLOTS * WIDTH // 2,
            transcendentals=total * ROWS * SLOTS // 2,
            bytes_accessed=total * ROWS * 2 * WIDTH * 2 + 3 * SLOTS * WIDTH * 8,
        ),
        name="attend",
    )(par, pos, *operands)


def project_body(index_ref, gq_ref, w_ref, out_ref):
    grad_query = gq_ref[...]
    width = grad_query.shape[1]
    for i in range(X):
        block = pl.ds(pl.multiple_of(index_ref[i] * width, width), width)
        out_ref[i] = lax.dot_general(
            grad_query,
            w_ref[block, :],
            (((1,), (1,)), ((), ())),
            preferred_element_type=jnp.float32,
        ).astype(jnp.bfloat16)


def project(index, grad_query, w_query):
    vmem = pl.BlockSpec(memory_space=pltpu.VMEM)
    return pl.pallas_call(
        project_body,
        in_specs=[pl.BlockSpec(memory_space=pltpu.SMEM), vmem, vmem],
        out_specs=vmem,
        out_shape=jax.ShapeDtypeStruct((X, ROWS, grad_query.shape[1]), jnp.bfloat16),
        compiler_params=pltpu.CompilerParams(vmem_limit_bytes=16 << 20),
        name="project",
    )(index, grad_query, w_query)


def exchange(value, axis, mask):
    count = lax.axis_size(axis)
    return lax.ppermute(value, axis, [(i, i ^ mask) for i in range(count)])


def add(a, b):
    return (a.astype(jnp.float32) + b.astype(jnp.float32)).astype(jnp.bfloat16)


def reduce_heads(grad_query, w_query, d_out):
    x_id = lax.axis_index("x")
    core = lax.axis_index("core")
    order = jnp.arange(X, dtype=jnp.int32)
    order = x_id ^ (order ^ (order >> 1))
    sent = exchange(project(order * C + (1 - core), grad_query, w_query), "core", 1)
    held = add(project(order * C + core, grad_query, w_query), sent)
    total = held[0].astype(jnp.float32) + d_out.astype(jnp.float32)
    for i, mask in ((3, 2), (1, 1), (2, 3)):
        total = total + exchange(held[i], "x", mask).astype(jnp.float32)
    return total.astype(jnp.bfloat16)


def shards(queries, keys, values, d_attn, d_out, w_query, prefix_len):
    y_id = lax.axis_index("y")
    z_id = lax.axis_index("z")
    section = y_id * Z + z_id
    base = section * ROWS
    lo = jnp.maximum(base - prefix_len[section], 0)
    par = jnp.where(jnp.arange(2) == 0, base, lo).astype(jnp.int32)
    q, g = queries, d_attn

    mine = lax.all_gather(jnp.concatenate([keys, values], axis=1), "y", axis=0)

    up = [(z, (z + 1) % Z) for z in range(Z)]
    down = [(z, (z - 1) % Z) for z in range(Z)]

    turn = jnp.arange(Z * Y, dtype=jnp.int32)
    hop = turn // Y
    hop = jnp.where(hop % 2 == 1, (hop + 1) // 2, Z - hop // 2)
    pos = ((z_id + Z - hop) % Z + turn % Y * Z) * ROWS

    half = Z // 2
    below = above = mine
    arrays, done = [mine], 0
    state = None
    for step in range(1, half + 1):
        last = step == half
        below = lax.ppermute(below[: Y // 2] if last else below, "z", up)
        above = lax.ppermute(above[Y // 2 :] if last else above, "z", down)
        if step % 2 == 0 or step == half - 1:
            state = attention(par, pos, done, q, g, arrays, state, False)
            done += sum(a.shape[0] for a in arrays)
            arrays = []
        arrays += [below, above]
    state = attention(par, pos, done, q, g, arrays, state, True)
    hidden = reduce_heads(state, w_query, d_out)
    return lax.ppermute(hidden, ("y", "z"), [(i + 1, i) for i in range(Y * Z - 1)])


def solution(mesh):
    fine = Mesh(mesh.devices.reshape(Y, Z, X, C), ("y", "z", "x", "core"))
    split = P(("y", "z"), ("x", "core"))
    placed = (split, split, split, split, split, P(None, ("x", "core")), P())

    return jax.shard_map(shards, mesh=fine, in_specs=placed, out_specs=split, check_vma=False)
```

```python
import functools
import math

import jax
import jax.numpy as jnp
from jax import lax
from jax.experimental import pallas as pl
from jax.experimental.pallas import tpu as pltpu
from jax.sharding import Mesh, PartitionSpec as P


ROWS = 192
SEG = 96
PAIR = 2
WIDTH = 128
HEADS = 4
SLOTS = HEADS * ROWS
LOW = -1e30
SLACK = 8.0
SCALE = WIDTH ** -0.5
Y, Z, X, C = 4, 16, 4, 2


def attend(counts, group, offset, first, last, par_ref, pos_ref, *refs):
    refs = list(refs)
    qg_refs = refs[:2]
    kv_refs = refs[2 : 2 + len(counts)]
    refs = refs[2 + len(counts) :]
    if not first:
        sw_in, sp_in, st_in = refs[:3]
        refs = refs[3:]
    outs = refs[:3]
    slot_pos, buf, q_s, g_s, m_s, w_s, p_s = refs[3:]

    for t, qg_ref in enumerate(qg_refs):
        for h in range(HEADS):
            rows = pl.ds(h * ROWS, ROWS)
            scaled = qg_ref[:, pl.ds(h * WIDTH, WIDTH)].astype(jnp.float32) * (
                SCALE * math.log2(math.e)
            )
            high = scaled.astype(jnp.bfloat16)
            q_s[t, rows, :WIDTH] = high
            q_s[t, rows, WIDTH:] = (scaled - high.astype(jnp.float32)).astype(jnp.bfloat16)
            g_s[t, rows, :] = qg_ref[:, pl.ds((HEADS + h) * WIDTH, WIDTH)]
        if first:
            m_s[t] = jnp.full((SLOTS, WIDTH), LOW, jnp.float32)
            w_s[t] = jnp.zeros((SLOTS, 2 * WIDTH), jnp.float32)
            p_s[t] = jnp.zeros((SLOTS, 2 * WIDTH), jnp.float32)
        else:
            st = st_in[t]
            shape = (SLOTS, WIDTH)
            m_s[t] = jnp.broadcast_to(st[:, 0:1], shape)
            p_s[t, :, :WIDTH] = sp_in[t]
            p_s[t, :, WIDTH:] = jnp.broadcast_to(st[:, 64:65], shape)
            w_s[t, :, :WIDTH] = sw_in[t]
            w_s[t, :, WIDTH:] = jnp.broadcast_to(st[:, 127:128], shape)

    @pl.loop(0, PAIR)
    def _(t):
        sweep(
            counts, group, offset, par_ref[2 * t], par_ref[2 * t + 1], pos_ref, kv_refs,
            slot_pos, buf, q_s.at[t], g_s.at[t], m_s.at[t], w_s.at[t], p_s.at[t],
        )

    lane = lax.broadcasted_iota(jnp.int32, (SLOTS, WIDTH), 1)
    for t in range(PAIR):
        if not last:
            sw_out, sp_out, st_out = outs
            sw_out[t] = w_s[t, :, :WIDTH]
            sp_out[t] = p_s[t, :, :WIDTH]
            st_out[t] = jnp.where(
                lane < 43, m_s[t], jnp.where(lane < 86, p_s[t, :, WIDTH:], w_s[t, :, WIDTH:])
            )
            continue
        kept, sent, sent_stats = outs
        l = p_s[t, :, WIDTH:]
        some = l > 0.0
        l = jnp.where(some, l, 1.0)
        delta = w_s[t, :, WIDTH:] / l
        key_mean = p_s[t, :, :WIDTH] / l
        centred = w_s[t, :, :WIDTH] / l - delta * key_mean
        weight = jnp.where(some, m_s[t] + jnp.log2(l), LOW)
        if t == 0:
            kept[0], kept[1], kept[2], kept[3] = centred, key_mean, weight, delta
        else:
            sent[0] = centred.astype(jnp.bfloat16)
            sent[1] = key_mean.astype(jnp.bfloat16)
            row = lax.broadcasted_iota(jnp.int32, (8, SLOTS), 0)
            sent_stats[...] = jnp.where(row < 4, weight.T[:8], delta.T[:8])


def merge_body(kept, came, came_stats, out_ref):
    stats = jnp.concatenate([came_stats[...]] * (WIDTH // 8), axis=0).T
    weight_b, delta_b = stats[:, 0:1], stats[:, 4:5]
    weight_a, delta_a = kept[2], kept[3]
    top = jnp.maximum(weight_a, weight_b)
    a = jnp.exp2(weight_a - top)
    b = jnp.exp2(weight_b - top)
    total = a + b
    a = a / total
    b = b / total
    delta = a * delta_a + b * delta_b
    grad = a * (kept[0] + (delta_a - delta) * kept[1])
    grad += b * (came[0].astype(jnp.float32) + (delta_b - delta) * came[1].astype(jnp.float32))
    grad = grad * SCALE
    for h in range(HEADS):
        out_ref[:, pl.ds(h * WIDTH, WIDTH)] = grad[h * ROWS : (h + 1) * ROWS].astype(jnp.bfloat16)


def merge(kept, came, came_stats):
    vmem = pl.BlockSpec(memory_space=pltpu.VMEM)
    return pl.pallas_call(
        merge_body,
        in_specs=[vmem] * 3,
        out_specs=vmem,
        out_shape=jax.ShapeDtypeStruct((ROWS, HEADS * WIDTH), jnp.bfloat16),
        compiler_params=pltpu.CompilerParams(vmem_limit_bytes=16 << 20),
        name="merge",
    )(kept, came, came_stats)


def sweep(
    counts, group, offset, base, lo, pos_ref, kv_refs, slot_pos, buf, q_s, g_s, m_s, w_s, p_s
):
    def collect(used, chosen_of):
        at = offset
        for ref, n in zip(kv_refs, counts):

            def place(j, slot, ref=ref, at=at):
                p = pos_ref[at + j]
                chosen = chosen_of(p)

                @pl.when(chosen)
                def _():
                    buf[slot] = ref[j]
                    slot_pos[slot] = p

                return slot + chosen.astype(jnp.int32)

            used = lax.fori_loop(0, n, place, used)
            at += n
        return used

    full = collect(jnp.int32(0), lambda p: (p >= lo) & (p < base))
    used = collect(
        full, lambda p: (p + SEG > lo) & (p < base + ROWS) & ((p < lo) | (p >= base))
    )
    groups = (used + group - 1) // group
    for j in range(group - 1):

        @pl.when(used + j < groups * group)
        def _():
            buf[used + j] = jnp.zeros((SEG, 2 * WIDTH), jnp.bfloat16)
            slot_pos[used + j] = jnp.int32(1 << 30)

    contract = (((1,), (1,)), ((), ()))

    def visit(g, rows, masked):
        start = g * group
        kv = jnp.concatenate([buf[start + j] for j in range(group)], axis=0)
        k, v = kv[:, :WIDTH], kv[:, WIDTH:]
        kk = jnp.concatenate([k, k], axis=1)
        k1 = jnp.concatenate([k, jnp.ones_like(k)], axis=1)
        s = lax.dot_general(q_s[rows, :], kk, contract, preferred_element_type=jnp.float32)
        if masked:
            lane = lax.broadcasted_iota(jnp.int32, (1, SEG), 1)
            key_at = jnp.concatenate([lane + slot_pos[start + j] for j in range(group)], axis=1)
            row = lax.broadcasted_iota(jnp.int32, (ROWS, group * SEG), 0) + base
            inside = (key_at >= lo) & (key_at <= row)
            s = jnp.where(inside, s, LOW)
        top = jnp.max(s, axis=1, keepdims=True)

        @pl.when(jnp.max(top - m_s[rows, 0:1]) > SLACK)
        def _():
            old = m_s[rows, :]
            new = jnp.maximum(old, top)
            factor = jnp.exp2(old - new)[:, 0:1]
            m_s[rows, :] = new
            w_s[rows, :] = w_s[rows, :] * factor
            p_s[rows, :] = p_s[rows, :] * factor

        prob = jnp.exp2(s - m_s[rows, 0:1])
        if masked:
            prob = jnp.where(inside, prob, 0.0)
        dp = lax.dot_general(g_s[rows, :], v, contract, preferred_element_type=jnp.float32)
        w_s[rows, :] += jnp.dot(
            (prob * dp).astype(jnp.bfloat16), k1, preferred_element_type=jnp.float32
        )
        p_s[rows, :] += jnp.dot(prob.astype(jnp.bfloat16), k1, preferred_element_type=jnp.float32)

    @pl.loop(0, groups)
    def _(g):
        whole = (g + 1) * group <= full
        pl.when(whole)(lambda: visit(g, pl.ds(0, SLOTS), False))

        @pl.when(jnp.logical_not(whole))
        def _():
            @pl.loop(0, HEADS)
            def _(h):
                visit(g, pl.ds(pl.multiple_of(h * ROWS, ROWS), ROWS), True)


def attention(par, pos, offset, qg, arrays, state, last):
    counts = tuple(a.shape[0] for a in arrays)
    first = state is None
    total = sum(counts)
    group = {4: 4, 12: 6}.get(total, 8)
    shape = jax.ShapeDtypeStruct((PAIR, SLOTS, WIDTH), jnp.float32)
    out_shape = [shape] * 3
    if last:
        out_shape = [
            jax.ShapeDtypeStruct((4, SLOTS, WIDTH), jnp.float32),
            jax.ShapeDtypeStruct((2, SLOTS, WIDTH), jnp.bfloat16),
            jax.ShapeDtypeStruct((8, SLOTS), jnp.float32),
        ]
    operands = [*qg, *arrays] + ([] if first else list(state))
    vmem = pl.BlockSpec(memory_space=pltpu.VMEM)
    smem = pl.BlockSpec(memory_space=pltpu.SMEM)
    return pl.pallas_call(
        functools.partial(attend, counts, group, offset, first, last),
        in_specs=[smem, smem] + [vmem] * len(operands),
        out_specs=[vmem] * 3,
        out_shape=out_shape,
        scratch_shapes=[
            pltpu.SMEM((total + group,), jnp.int32),
            pltpu.VMEM((total + group, SEG, 2 * WIDTH), jnp.bfloat16),
            pltpu.VMEM((PAIR, SLOTS, 2 * WIDTH), jnp.bfloat16),
            pltpu.VMEM((PAIR, SLOTS, WIDTH), jnp.bfloat16),
            pltpu.VMEM((PAIR, SLOTS, WIDTH), jnp.float32),
            pltpu.VMEM((PAIR, SLOTS, 2 * WIDTH), jnp.float32),
            pltpu.VMEM((PAIR, SLOTS, 2 * WIDTH), jnp.float32),
        ],
        compiler_params=pltpu.CompilerParams(vmem_limit_bytes=20 << 20),
        cost_estimate=pl.CostEstimate(
            flops=8 * total * SEG * SLOTS * WIDTH,
            transcendentals=total * SEG * SLOTS,
            bytes_accessed=total * SEG * 2 * WIDTH * 2 + 6 * SLOTS * WIDTH * 8,
        ),
        name="attend",
    )(par, pos, *operands)


def project_body(index_ref, gq_ref, w_ref, out_ref):
    grad_query = gq_ref[...]
    width = grad_query.shape[1]
    for i in range(X):
        block = pl.ds(pl.multiple_of(index_ref[i] * width, width), width)
        out_ref[i] = lax.dot_general(
            grad_query,
            w_ref[block, :],
            (((1,), (1,)), ((), ())),
            preferred_element_type=jnp.float32,
        ).astype(jnp.bfloat16)


def project(index, grad_query, w_query):
    vmem = pl.BlockSpec(memory_space=pltpu.VMEM)
    return pl.pallas_call(
        project_body,
        in_specs=[pl.BlockSpec(memory_space=pltpu.SMEM), vmem, vmem],
        out_specs=vmem,
        out_shape=jax.ShapeDtypeStruct((X, ROWS, grad_query.shape[1]), jnp.bfloat16),
        compiler_params=pltpu.CompilerParams(vmem_limit_bytes=16 << 20),
        name="project",
    )(index, grad_query, w_query)


def exchange(value, axis, mask):
    count = lax.axis_size(axis)
    return lax.ppermute(value, axis, [(i, i ^ mask) for i in range(count)])


def add(a, b):
    return (a.astype(jnp.float32) + b.astype(jnp.float32)).astype(jnp.bfloat16)


def reduce_heads(grad_query, w_query, d_out):
    x_id = lax.axis_index("x")
    core = lax.axis_index("core")
    order = jnp.arange(X, dtype=jnp.int32)
    order = x_id ^ (order ^ (order >> 1))
    sent = exchange(project(order * C + (1 - core), grad_query, w_query), "core", 1)
    held = add(project(order * C + core, grad_query, w_query), sent)
    total = held[0].astype(jnp.float32) + d_out.astype(jnp.float32)
    for i, mask in ((3, 2), (1, 1), (2, 3)):
        total = total + exchange(held[i], "x", mask).astype(jnp.float32)
    return total.astype(jnp.bfloat16)


def shards(queries, keys, values, d_attn, d_out, w_query, prefix_len):
    y_id = lax.axis_index("y")
    z_id = lax.axis_index("z")
    base = (y_id * Z + z_id) * ROWS
    other = ((Y - 1 - y_id) * Z + z_id) * ROWS
    low = jnp.maximum(base - prefix_len[base // ROWS], 0)
    other_low = jnp.maximum(other - prefix_len[other // ROWS], 0)
    entry = jnp.arange(2 * PAIR)
    par = jnp.where(entry < 2, jnp.where(entry == 0, base, low), jnp.where(entry == 2, other, other_low))
    par = par.astype(jnp.int32)
    part = (y_id >= Y // 2).astype(jnp.int32) * SEG

    qg = jnp.concatenate([queries, d_attn], axis=1)
    mirror = [(y, Y - 1 - y) for y in range(Y)]
    qg = (qg, lax.ppermute(qg, "y", mirror))

    mine = lax.all_gather(jnp.concatenate([keys, values], axis=1), "y", axis=0)
    mine = lax.dynamic_slice_in_dim(mine, part, SEG, axis=1)

    up = [(z, (z + 1) % Z) for z in range(Z)]
    down = [(z, (z - 1) % Z) for z in range(Z)]

    turn = jnp.arange(Z * Y, dtype=jnp.int32)
    hop = turn // Y
    hop = jnp.where(hop % 2 == 1, (hop + 1) // 2, Z - hop // 2)
    pos = ((z_id + Z - hop) % Z + turn % Y * Z) * ROWS + part

    half = Z // 2
    below = above = mine
    arrays, done = [mine], 0
    state = None
    for step in range(1, half + 1):
        last = step == half
        below = lax.ppermute(below[: Y // 2] if last else below, "z", up)
        above = lax.ppermute(above[Y // 2 :] if last else above, "z", down)
        if step % 2 == 0 or step == half - 1:
            state = attention(par, pos, done, qg, arrays, state, False)
            done += sum(a.shape[0] for a in arrays)
            arrays = []
        arrays += [below, above]
    kept, sent, stats = attention(par, pos, done, qg, arrays, state, True)
    came = lax.ppermute(sent, "y", mirror)
    came_stats = lax.ppermute(stats, "y", mirror)
    hidden = reduce_heads(merge(kept, came, came_stats), w_query, d_out)
    return lax.ppermute(hidden, ("y", "z"), [(i + 1, i) for i in range(Y * Z - 1)])


def solution(mesh):
    fine = Mesh(mesh.devices.reshape(Y, Z, X, C), ("y", "z", "x", "core"))
    split = P(("y", "z"), ("x", "core"))
    placed = (split, split, split, split, split, P(None, ("x", "core")), P())

    return jax.shard_map(shards, mesh=fine, in_specs=placed, out_specs=split, check_vma=False)
```

```python
import functools
import math

import jax
import jax.numpy as jnp
from jax import lax
from jax.experimental import pallas as pl
from jax.experimental.pallas import tpu as pltpu
from jax.sharding import Mesh, PartitionSpec as P


ROWS = 192
WIDTH = 128
HEADS = 4
SLOTS = HEADS * ROWS
LOW = -1e30
SLACK = 8.0
REST = 4
SCALE = WIDTH ** -0.5
Y, Z, X, C = 4, 16, 4, 2


def attend(counts, group, offset, first, last, par_ref, pos_ref, *refs):
    refs = list(refs)
    q_ref, g_ref = refs[:2]
    kv_refs = refs[2 : 2 + len(counts)]
    refs = refs[2 + len(counts) :]
    if not first:
        sw_in, sp_in, st_in = refs[:3]
        refs = refs[3:]
    outs = refs[: 1 if last else 3]
    slot_pos, buf, q_s, g_s, m_s, w_s, p_s = refs[1 if last else 3 :]
    base = par_ref[0]
    lo = par_ref[1]

    for h in range(HEADS):
        rows = pl.ds(h * ROWS, ROWS)
        cols = pl.ds(h * WIDTH, WIDTH)
        scaled = q_ref[:, cols].astype(jnp.float32) * (SCALE * math.log2(math.e))
        high = scaled.astype(jnp.bfloat16)
        q_s[rows, :WIDTH] = high
        q_s[rows, WIDTH:] = (scaled - high.astype(jnp.float32)).astype(jnp.bfloat16)
        g_s[rows, :] = g_ref[:, cols]
    if first:
        m_s[...] = jnp.full((SLOTS, WIDTH), LOW, jnp.float32)
        w_s[...] = jnp.zeros((SLOTS, 2 * WIDTH), jnp.float32)
        p_s[...] = jnp.zeros((SLOTS, 2 * WIDTH), jnp.float32)
    else:
        st = st_in[...]
        shape = (SLOTS, WIDTH)
        m_s[...] = jnp.broadcast_to(st[:, 0:1], shape)
        p_s[:, :WIDTH] = sp_in[...]
        p_s[:, WIDTH:] = jnp.broadcast_to(st[:, 64:65], shape)
        w_s[:, :WIDTH] = sw_in[...]
        w_s[:, WIDTH:] = jnp.broadcast_to(st[:, 127:128], shape)

    def collect(used, chosen_of):
        at = offset
        for ref, n in zip(kv_refs, counts):

            def place(j, slot, ref=ref, at=at):
                p = pos_ref[at + j]
                chosen = chosen_of(p)

                @pl.when(chosen)
                def _():
                    buf[slot] = ref[j]
                    slot_pos[slot] = p

                return slot + chosen.astype(jnp.int32)

            used = lax.fori_loop(0, n, place, used)
            at += n
        return used

    full = collect(jnp.int32(0), lambda p: (p >= lo) & (p < base))
    used = collect(
        full, lambda p: (p + ROWS > lo) & (p <= base) & ((p < lo) | (p == base))
    )
    wholes = full // group
    head = wholes * group
    rests = (used - head + REST - 1) // REST
    for j in range(REST - 1):

        @pl.when(used + j < head + rests * REST)
        def _():
            buf[used + j] = jnp.zeros((ROWS, 2 * WIDTH), jnp.bfloat16)
            slot_pos[used + j] = jnp.int32(1 << 30)

    contract = (((1,), (1,)), ((), ()))

    def visit(start, size, rows, masked):
        kv = jnp.concatenate([buf[start + j] for j in range(size)], axis=0)
        k, v = kv[:, :WIDTH], kv[:, WIDTH:]
        kk = jnp.concatenate([k, k], axis=1)
        k1 = jnp.concatenate([k, jnp.ones_like(k)], axis=1)
        s = lax.dot_general(q_s[rows, :], kk, contract, preferred_element_type=jnp.float32)
        if masked:
            lane = lax.broadcasted_iota(jnp.int32, (1, ROWS), 1)
            key_at = jnp.concatenate([lane + slot_pos[start + j] for j in range(size)], axis=1)
            row = lax.broadcasted_iota(jnp.int32, (ROWS, size * ROWS), 0) + base
            inside = (key_at >= lo) & (key_at <= row)
            s = jnp.where(inside, s, LOW)
        top = jnp.max(s, axis=1, keepdims=True)

        @pl.when(jnp.max(top - m_s[rows, 0:1]) > SLACK)
        def _():
            old = m_s[rows, :]
            new = jnp.maximum(old, top)
            factor = jnp.exp2(old - new)[:, 0:1]
            m_s[rows, :] = new
            w_s[rows, :] = w_s[rows, :] * factor
            p_s[rows, :] = p_s[rows, :] * factor

        prob = jnp.exp2(s - m_s[rows, 0:1])
        if masked:
            prob = jnp.where(inside, prob, 0.0)
        dp = lax.dot_general(g_s[rows, :], v, contract, preferred_element_type=jnp.float32)
        w_s[rows, :] += jnp.dot(
            (prob * dp).astype(jnp.bfloat16), k1, preferred_element_type=jnp.float32
        )
        p_s[rows, :] += jnp.dot(prob.astype(jnp.bfloat16), k1, preferred_element_type=jnp.float32)

    @pl.loop(0, wholes * 2)
    def _(i):
        rows = pl.ds(pl.multiple_of(i % 2 * (SLOTS // 2), SLOTS // 2), SLOTS // 2)
        visit(i // 2 * group, group, rows, False)

    @pl.loop(0, rests * HEADS)
    def _(i):
        rows = pl.ds(pl.multiple_of(i % HEADS * ROWS, ROWS), ROWS)
        visit(head + i // HEADS * REST, REST, rows, True)

    if last:
        l = p_s[:, WIDTH:]
        l = jnp.where(l > 0.0, l, 1.0)
        delta = w_s[:, WIDTH:] / l
        grad = (w_s[:, :WIDTH] - delta * p_s[:, :WIDTH]) / l * SCALE
        for h in range(HEADS):
            outs[0][:, pl.ds(h * WIDTH, WIDTH)] = grad[h * ROWS : (h + 1) * ROWS].astype(jnp.bfloat16)
    else:
        sw_out, sp_out, st_out = outs
        sw_out[...] = w_s[:, :WIDTH]
        sp_out[...] = p_s[:, :WIDTH]
        lane = lax.broadcasted_iota(jnp.int32, (SLOTS, WIDTH), 1)
        st_out[...] = jnp.where(
            lane < 43, m_s[...], jnp.where(lane < 86, p_s[:, WIDTH:], w_s[:, WIDTH:])
        )


def attention(par, pos, offset, q, g, arrays, state, last):
    counts = tuple(a.shape[0] for a in arrays)
    first = state is None
    total = sum(counts)
    group = min(total, 8)
    shape = jax.ShapeDtypeStruct((SLOTS, WIDTH), jnp.float32)
    out_shape = jax.ShapeDtypeStruct((ROWS, HEADS * WIDTH), jnp.bfloat16) if last else [shape] * 3
    operands = [q, g, *arrays] + ([] if first else list(state))
    vmem = pl.BlockSpec(memory_space=pltpu.VMEM)
    smem = pl.BlockSpec(memory_space=pltpu.SMEM)
    return pl.pallas_call(
        functools.partial(attend, counts, group, offset, first, last),
        in_specs=[smem, smem] + [vmem] * len(operands),
        out_specs=vmem if last else [vmem] * 3,
        out_shape=out_shape,
        scratch_shapes=[
            pltpu.SMEM((total + group,), jnp.int32),
            pltpu.VMEM((total + group, ROWS, 2 * WIDTH), jnp.bfloat16),
            pltpu.VMEM((SLOTS, 2 * WIDTH), jnp.bfloat16),
            pltpu.VMEM((SLOTS, WIDTH), jnp.bfloat16),
            pltpu.VMEM((SLOTS, WIDTH), jnp.float32),
            pltpu.VMEM((SLOTS, 2 * WIDTH), jnp.float32),
            pltpu.VMEM((SLOTS, 2 * WIDTH), jnp.float32),
        ],
        compiler_params=pltpu.CompilerParams(vmem_limit_bytes=24 << 20),
        cost_estimate=pl.CostEstimate(
            flops=8 * total * ROWS * SLOTS * WIDTH // 2,
            transcendentals=total * ROWS * SLOTS // 2,
            bytes_accessed=total * ROWS * 2 * WIDTH * 2 + 3 * SLOTS * WIDTH * 8,
        ),
        name="attend",
    )(par, pos, *operands)


def project_body(index_ref, gq_ref, w_ref, out_ref):
    grad_query = gq_ref[...]
    width = grad_query.shape[1]
    for i in range(X):
        block = pl.ds(pl.multiple_of(index_ref[i] * width, width), width)
        out_ref[i] = lax.dot_general(
            grad_query,
            w_ref[block, :],
            (((1,), (1,)), ((), ())),
            preferred_element_type=jnp.float32,
        ).astype(jnp.bfloat16)


def project(index, grad_query, w_query):
    vmem = pl.BlockSpec(memory_space=pltpu.VMEM)
    return pl.pallas_call(
        project_body,
        in_specs=[pl.BlockSpec(memory_space=pltpu.SMEM), vmem, vmem],
        out_specs=vmem,
        out_shape=jax.ShapeDtypeStruct((X, ROWS, grad_query.shape[1]), jnp.bfloat16),
        compiler_params=pltpu.CompilerParams(vmem_limit_bytes=16 << 20),
        name="project",
    )(index, grad_query, w_query)


def exchange(value, axis, mask):
    count = lax.axis_size(axis)
    return lax.ppermute(value, axis, [(i, i ^ mask) for i in range(count)])


def add(a, b):
    return (a.astype(jnp.float32) + b.astype(jnp.float32)).astype(jnp.bfloat16)


def reduce_heads(grad_query, w_query, d_out):
    x_id = lax.axis_index("x")
    core = lax.axis_index("core")
    order = jnp.arange(X, dtype=jnp.int32)
    order = x_id ^ (order ^ (order >> 1))
    sent = exchange(project(order * C + (1 - core), grad_query, w_query), "core", 1)
    held = add(project(order * C + core, grad_query, w_query), sent)
    total = held[0].astype(jnp.float32) + d_out.astype(jnp.float32)
    for i, mask in ((3, 2), (1, 1), (2, 3)):
        total = total + exchange(held[i], "x", mask).astype(jnp.float32)
    return total.astype(jnp.bfloat16)


def shards(queries, keys, values, d_attn, d_out, w_query, prefix_len):
    y_id = lax.axis_index("y")
    z_id = lax.axis_index("z")
    section = y_id * Z + z_id
    base = section * ROWS
    lo = jnp.maximum(base - prefix_len[section], 0)
    par = jnp.where(jnp.arange(2) == 0, base, lo).astype(jnp.int32)
    q, g = queries, d_attn

    mine = lax.all_gather(jnp.concatenate([keys, values], axis=1), "y", axis=0)

    up = [(z, (z + 1) % Z) for z in range(Z)]
    down = [(z, (z - 1) % Z) for z in range(Z)]

    turn = jnp.arange(Z * Y, dtype=jnp.int32)
    hop = turn // Y
    hop = jnp.where(hop % 2 == 1, (hop + 1) // 2, Z - hop // 2)
    pos = ((z_id + Z - hop) % Z + turn % Y * Z) * ROWS

    half = Z // 2
    below = above = mine
    arrays, done = [mine], 0
    state = None
    for step in range(1, half + 1):
        last = step == half
        below = lax.ppermute(below[: Y // 2] if last else below, "z", up)
        above = lax.ppermute(above[Y // 2 :] if last else above, "z", down)
        state = attention(par, pos, done, q, g, arrays, state, False)
        done += sum(a.shape[0] for a in arrays)
        arrays = []
        arrays += [below, above]
    state = attention(par, pos, done, q, g, arrays, state, True)
    hidden = reduce_heads(state, w_query, d_out)
    return lax.ppermute(hidden, ("y", "z"), [(i + 1, i) for i in range(Y * Z - 1)])


def solution(mesh):
    fine = Mesh(mesh.devices.reshape(Y, Z, X, C), ("y", "z", "x", "core"))
    split = P(("y", "z"), ("x", "core"))
    placed = (split, split, split, split, split, P(None, ("x", "core")), P())

    return jax.shard_map(shards, mesh=fine, in_specs=placed, out_specs=split, check_vma=False)
```

```python
import functools
import math

import jax
import jax.numpy as jnp
from jax import lax
from jax.experimental import pallas as pl
from jax.experimental.pallas import tpu as pltpu
from jax.sharding import Mesh, PartitionSpec as P


ROWS = 192
WIDTH = 128
HEADS = 4
SLOTS = HEADS * ROWS
LOW = -1e30
SLACK = 8.0
REST = 2
SCALE = WIDTH ** -0.5
Y, Z, X, C = 4, 16, 4, 2


def attend(counts, group, offset, first, last, par_ref, pos_ref, *refs):
    refs = list(refs)
    q_ref, g_ref = refs[:2]
    kv_refs = refs[2 : 2 + len(counts)]
    refs = refs[2 + len(counts) :]
    if not first:
        sw_in, sp_in, st_in = refs[:3]
        refs = refs[3:]
    outs = refs[: 1 if last else 3]
    slot_pos, buf, q_s, g_s, m_s, w_s, p_s = refs[1 if last else 3 :]
    base = par_ref[0]
    lo = par_ref[1]

    for h in range(HEADS):
        rows = pl.ds(h * ROWS, ROWS)
        cols = pl.ds(h * WIDTH, WIDTH)
        scaled = q_ref[:, cols].astype(jnp.float32) * (SCALE * math.log2(math.e))
        high = scaled.astype(jnp.bfloat16)
        q_s[rows, :WIDTH] = high
        q_s[rows, WIDTH:] = (scaled - high.astype(jnp.float32)).astype(jnp.bfloat16)
        g_s[rows, :] = g_ref[:, cols]
    if first:
        m_s[...] = jnp.full((SLOTS, WIDTH), LOW, jnp.float32)
        w_s[...] = jnp.zeros((SLOTS, 2 * WIDTH), jnp.float32)
        p_s[...] = jnp.zeros((SLOTS, 2 * WIDTH), jnp.float32)
    else:
        st = st_in[...]
        shape = (SLOTS, WIDTH)
        m_s[...] = jnp.broadcast_to(st[:, 0:1], shape)
        p_s[:, :WIDTH] = sp_in[...]
        p_s[:, WIDTH:] = jnp.broadcast_to(st[:, 64:65], shape)
        w_s[:, :WIDTH] = sw_in[...]
        w_s[:, WIDTH:] = jnp.broadcast_to(st[:, 127:128], shape)

    def collect(used, chosen_of):
        at = offset
        for ref, n in zip(kv_refs, counts):

            def place(j, slot, ref=ref, at=at):
                p = pos_ref[at + j]
                chosen = chosen_of(p)

                @pl.when(chosen)
                def _():
                    buf[slot] = ref[j]
                    slot_pos[slot] = p

                return slot + chosen.astype(jnp.int32)

            used = lax.fori_loop(0, n, place, used)
            at += n
        return used

    full = collect(jnp.int32(0), lambda p: (p >= lo) & (p < base))
    used = collect(
        full, lambda p: (p + ROWS > lo) & (p <= base) & ((p < lo) | (p == base))
    )
    wholes = full // group
    fours = (full - wholes * group) // 4
    head = wholes * group + fours * 4
    rests = (used - head + REST - 1) // REST
    for j in range(REST - 1):

        @pl.when(used + j < head + rests * REST)
        def _():
            buf[used + j] = jnp.zeros((ROWS, 2 * WIDTH), jnp.bfloat16)
            slot_pos[used + j] = jnp.int32(1 << 30)

    contract = (((1,), (1,)), ((), ()))

    def visit(start, size, rows, masked):
        kv = jnp.concatenate([buf[start + j] for j in range(size)], axis=0)
        k, v = kv[:, :WIDTH], kv[:, WIDTH:]
        kk = jnp.concatenate([k, k], axis=1)
        k1 = jnp.concatenate([k, jnp.ones_like(k)], axis=1)
        s = lax.dot_general(q_s[rows, :], kk, contract, preferred_element_type=jnp.float32)
        if masked:
            lane = lax.broadcasted_iota(jnp.int32, (1, ROWS), 1)
            key_at = jnp.concatenate([lane + slot_pos[start + j] for j in range(size)], axis=1)
            row = lax.broadcasted_iota(jnp.int32, (ROWS, size * ROWS), 0) + base
            row = jnp.concatenate([row, row], axis=0)
            inside = (key_at >= lo) & (key_at <= row)
            s = jnp.where(inside, s, LOW)
        top = jnp.max(s, axis=1, keepdims=True)

        @pl.when(jnp.max(top - m_s[rows, 0:1]) > SLACK)
        def _():
            old = m_s[rows, :]
            new = jnp.maximum(old, top)
            factor = jnp.exp2(old - new)[:, 0:1]
            m_s[rows, :] = new
            w_s[rows, :] = w_s[rows, :] * factor
            p_s[rows, :] = p_s[rows, :] * factor

        prob = jnp.exp2(s - m_s[rows, 0:1])
        if masked:
            prob = jnp.where(inside, prob, 0.0)
        dp = lax.dot_general(g_s[rows, :], v, contract, preferred_element_type=jnp.float32)
        w_s[rows, :] += jnp.dot(
            (prob * dp).astype(jnp.bfloat16), k1, preferred_element_type=jnp.float32
        )
        p_s[rows, :] += jnp.dot(prob.astype(jnp.bfloat16), k1, preferred_element_type=jnp.float32)

    @pl.loop(0, wholes)
    def _(i):
        visit(i * group, group, pl.ds(0, SLOTS), False)

    def half(i):
        return pl.ds(pl.multiple_of(i % 2 * (SLOTS // 2), SLOTS // 2), SLOTS // 2)

    if group > 4:

        @pl.loop(0, fours * 2)
        def _(i):
            visit(wholes * group + i // 2 * 4, 4, half(i), False)

    @pl.loop(0, rests * 2)
    def _(i):
        visit(head + i // 2 * REST, REST, half(i), True)

    if last:
        l = p_s[:, WIDTH:]
        l = jnp.where(l > 0.0, l, 1.0)
        delta = w_s[:, WIDTH:] / l
        grad = (w_s[:, :WIDTH] - delta * p_s[:, :WIDTH]) / l * SCALE
        for h in range(HEADS):
            outs[0][:, pl.ds(h * WIDTH, WIDTH)] = grad[h * ROWS : (h + 1) * ROWS].astype(jnp.bfloat16)
    else:
        sw_out, sp_out, st_out = outs
        sw_out[...] = w_s[:, :WIDTH]
        sp_out[...] = p_s[:, :WIDTH]
        lane = lax.broadcasted_iota(jnp.int32, (SLOTS, WIDTH), 1)
        st_out[...] = jnp.where(
            lane < 43, m_s[...], jnp.where(lane < 86, p_s[:, WIDTH:], w_s[:, WIDTH:])
        )


def attention(par, pos, offset, q, g, arrays, state, last):
    counts = tuple(a.shape[0] for a in arrays)
    first = state is None
    total = sum(counts)
    group = min(total, 8)
    shape = jax.ShapeDtypeStruct((SLOTS, WIDTH), jnp.float32)
    out_shape = jax.ShapeDtypeStruct((ROWS, HEADS * WIDTH), jnp.bfloat16) if last else [shape] * 3
    operands = [q, g, *arrays] + ([] if first else list(state))
    vmem = pl.BlockSpec(memory_space=pltpu.VMEM)
    smem = pl.BlockSpec(memory_space=pltpu.SMEM)
    return pl.pallas_call(
        functools.partial(attend, counts, group, offset, first, last),
        in_specs=[smem, smem] + [vmem] * len(operands),
        out_specs=vmem if last else [vmem] * 3,
        out_shape=out_shape,
        scratch_shapes=[
            pltpu.SMEM((total + group,), jnp.int32),
            pltpu.VMEM((total + group, ROWS, 2 * WIDTH), jnp.bfloat16),
            pltpu.VMEM((SLOTS, 2 * WIDTH), jnp.bfloat16),
            pltpu.VMEM((SLOTS, WIDTH), jnp.bfloat16),
            pltpu.VMEM((SLOTS, WIDTH), jnp.float32),
            pltpu.VMEM((SLOTS, 2 * WIDTH), jnp.float32),
            pltpu.VMEM((SLOTS, 2 * WIDTH), jnp.float32),
        ],
        compiler_params=pltpu.CompilerParams(vmem_limit_bytes=24 << 20),
        cost_estimate=pl.CostEstimate(
            flops=8 * total * ROWS * SLOTS * WIDTH // 2,
            transcendentals=total * ROWS * SLOTS // 2,
            bytes_accessed=total * ROWS * 2 * WIDTH * 2 + 3 * SLOTS * WIDTH * 8,
        ),
        name="attend",
    )(par, pos, *operands)


def project_body(index_ref, gq_ref, w_ref, out_ref):
    grad_query = gq_ref[...]
    width = grad_query.shape[1]
    for i in range(X):
        block = pl.ds(pl.multiple_of(index_ref[i] * width, width), width)
        out_ref[i] = lax.dot_general(
            grad_query,
            w_ref[block, :],
            (((1,), (1,)), ((), ())),
            preferred_element_type=jnp.float32,
        ).astype(jnp.bfloat16)


def project(index, grad_query, w_query):
    vmem = pl.BlockSpec(memory_space=pltpu.VMEM)
    return pl.pallas_call(
        project_body,
        in_specs=[pl.BlockSpec(memory_space=pltpu.SMEM), vmem, vmem],
        out_specs=vmem,
        out_shape=jax.ShapeDtypeStruct((X, ROWS, grad_query.shape[1]), jnp.bfloat16),
        compiler_params=pltpu.CompilerParams(vmem_limit_bytes=16 << 20),
        name="project",
    )(index, grad_query, w_query)


def exchange(value, axis, mask):
    count = lax.axis_size(axis)
    return lax.ppermute(value, axis, [(i, i ^ mask) for i in range(count)])


def add(a, b):
    return (a.astype(jnp.float32) + b.astype(jnp.float32)).astype(jnp.bfloat16)


def reduce_heads(grad_query, w_query, d_out):
    x_id = lax.axis_index("x")
    core = lax.axis_index("core")
    order = jnp.arange(X, dtype=jnp.int32)
    order = x_id ^ (order ^ (order >> 1))
    sent = exchange(project(order * C + (1 - core), grad_query, w_query), "core", 1)
    held = add(project(order * C + core, grad_query, w_query), sent)
    total = held[0].astype(jnp.float32) + d_out.astype(jnp.float32)
    for i, mask in ((3, 2), (1, 1), (2, 3)):
        total = total + exchange(held[i], "x", mask).astype(jnp.float32)
    return total.astype(jnp.bfloat16)


def shards(queries, keys, values, d_attn, d_out, w_query, prefix_len):
    y_id = lax.axis_index("y")
    z_id = lax.axis_index("z")
    section = y_id * Z + z_id
    base = section * ROWS
    lo = jnp.maximum(base - prefix_len[section], 0)
    par = jnp.where(jnp.arange(2) == 0, base, lo).astype(jnp.int32)
    q, g = queries, d_attn

    mine = lax.all_gather(jnp.concatenate([keys, values], axis=1), "y", axis=0)

    up = [(z, (z + 1) % Z) for z in range(Z)]
    down = [(z, (z - 1) % Z) for z in range(Z)]

    turn = jnp.arange(Z * Y, dtype=jnp.int32)
    hop = turn // Y
    hop = jnp.where(hop % 2 == 1, (hop + 1) // 2, Z - hop // 2)
    pos = ((z_id + Z - hop) % Z + turn % Y * Z) * ROWS

    half = Z // 2
    below = above = mine
    arrays, done = [mine], 0
    state = None
    for step in range(1, half + 1):
        last = step == half
        below = lax.ppermute(below[: Y // 2] if last else below, "z", up)
        above = lax.ppermute(above[Y // 2 :] if last else above, "z", down)
        if step % 2 == 0:
            state = attention(par, pos, done, q, g, arrays, state, False)
            done += sum(a.shape[0] for a in arrays)
            arrays = []
        arrays += [below, above]
    state = attention(par, pos, done, q, g, arrays, state, True)
    hidden = reduce_heads(state, w_query, d_out)
    return lax.ppermute(hidden, ("y", "z"), [(i + 1, i) for i in range(Y * Z - 1)])


def solution(mesh):
    fine = Mesh(mesh.devices.reshape(Y, Z, X, C), ("y", "z", "x", "core"))
    split = P(("y", "z"), ("x", "core"))
    placed = (split, split, split, split, split, P(None, ("x", "core")), P())

    return jax.shard_map(shards, mesh=fine, in_specs=placed, out_specs=split, check_vma=False)
```
